32 devices in a mesh: groups: 2 (over x), tm: 16 (over z, y, core).
Axes of the slice: x: 2, y: 2, z: 4, core: 2. Of those that a mesh axis runs over, the one named last changes fastest.
Arguments:
- frames: float32 [64, 196, 1024], P(('groups', 'tm')), parts along dimension 0, may hold values from -6 to 6
- cotangent: float32 [64, 196, 1024], P(('groups', 'tm')), parts along dimension 0, may hold values from -6 to 6
- reduce_weight: float32 [1024, 256], replicated, may hold values from -0.1875 to 0.1875
- spatial_weight: float32 [2304, 256], replicated, may hold values from -0.125 to 0.125
- expand_weight: float32 [1024, 256], replicated, may hold values from -0.375 to 0.375
- reduce_scale: float32 [256], replicated, may hold values from 0.5 to 2
- reduce_bias: float32 [256], replicated, may hold values from -0.8 to 0.8
- spatial_scale: float32 [256], replicated, may hold values from 0.5 to 2
- spatial_bias: float32 [256], replicated, may hold values from -0.8 to 0.8
- expand_scale: float32 [1024], replicated, may hold values from 0.5 to 2
- expand_bias: float32 [1024], replicated, may hold values from -0.8 to 0.8
Outputs:
- block_out: float32 [64, 196, 1024], P(('groups', 'tm')), parts along dimension 0
- grad_frames: float32 [64, 196, 1024], P(('groups', 'tm')), parts along dimension 0
- grad_reduce: float32 [2048, 256], P(('groups', 'tm')), parts along dimension 0
- grad_spatial: float32 [4608, 256], P(('groups', 'tm')), parts along dimension 0
- grad_expand: float32 [2048, 256], P(('groups', 'tm')), parts along dimension 0
The draws below stay inside these ranges and needn't reach their ends.
There are 2 independent parts, one for each index of `groups`. The reference program is written for one: setup_inputs(seed, part) draws one part's arguments, and reference() takes and returns one part's arrays. A program takes and returns all parts, laid end to end along the dimension named above; an argument that names none is the same for every part. Nothing has to cross between parts.
All inputs are finite; a program needn't handle non-finite values.
Results may differ from the reference program's by a relative error of at most 0.00007.
Values sent between devices are 32-bit elements; how exact they have to be, the bound alone decides.
No kernel may reach another device: no remote copies, remote signals or barrier semaphores. Data moves between devices by JAX's collectives and lax.ppermute only.
A program may use at most 128 MiB of HBM per device.

```python
import math
import jax
import jax.numpy as jnp
from jax import lax

CIN = 1024
MID = 256
SIDE = 14
HW = 196
FRAMES = 32


def raised(drawn, stream_key, source, target, blocks, factor):
    owner, partner = [(jnp.arange(drawn.shape[axis_at]) // (drawn.shape[axis_at] // blocks)).reshape([-1 if axis == axis_at else 1 for axis in range(drawn.ndim)]) for axis_at in (source, target)]
    chosen = jax.random.permutation(stream_key, blocks)[partner]
    strong = (owner == chosen) | (owner == (partner + blocks // 2) % blocks)
    return jnp.where(strong, factor * drawn, drawn)


def block_scale(key, shape, shards, least, largest):
    def one(position, shards_of):
        heights = jax.random.uniform(jax.random.fold_in(jax.random.fold_in(key, 6), position), (shards_of,), jnp.float32, least / len(shards), largest / len(shards))
        return jnp.repeat(jnp.exp(heights), shape[position] // shards_of).reshape((-1,) + (1,) * (len(shape) - position - 1))

    level = one(*shards[0])
    for cut in shards[1:]:
        level = level * one(*cut)
    return level


def noise(own_key, extent, width, bound, shards=(), dtype=jnp.bfloat16):
    drawn = jax.random.normal(own_key, extent, jnp.float32) * width
    if len(shards) > 0:
        drawn = block_scale(own_key, extent, shards, -0.22, 0.18) * drawn
    return jnp.clip(drawn, min=-bound, max=bound).astype(dtype)


def bell_draw_with(key, extent, spread, limit, cuts, heavy, dtype=jnp.bfloat16):
    entries = spread * jax.random.normal(key, extent, jnp.float32)
    if cuts:
        entries = entries * block_scale(key, extent, cuts, -0.22, 0.18)
    return jnp.clip(raised(entries, jax.random.fold_in(key, 3), *heavy), -limit, limit).astype(dtype)


def setup_inputs(seed: int = 0, part: int = 0) -> dict:
    seeds = jax.random.split(jax.random.key(seed), 12)
    part_keys = jax.random.split(jax.random.fold_in(seeds[11], part), 12)
    frames = noise(part_keys[0], (FRAMES, HW, CIN), 1.0, 6.0, ((0, 16),), jnp.float32)
    cotangent = bell_draw_with(part_keys[1], (FRAMES, HW, CIN), 1.0, 6.0, ((0, 16),), (0, 2, 16, 2.0), jnp.float32)
    reduce_weight = noise(seeds[2], (CIN, MID), CIN ** -0.5, 0.1875, (), jnp.float32)
    spatial_weight = noise(seeds[3], (9 * MID, MID), (9 * MID) ** -0.5, 0.125, (), jnp.float32)
    expand_weight = noise(seeds[4], (CIN, MID), MID ** -0.5, 0.375, (), jnp.float32)
    reduce_scale = jnp.clip(jnp.exp(jax.random.uniform(seeds[5], (MID,), jnp.float32, math.log(0.5), math.log(2.0))), 0.5, 2.0)
    reduce_bias = jnp.clip(jax.random.uniform(seeds[6], (MID,), jnp.float32, -0.8, 0.8), -0.8, 0.8)
    spatial_scale = jnp.clip(jnp.exp(jax.random.uniform(seeds[7], (MID,), jnp.float32, math.log(0.5), math.log(2.0))), 0.5, 2.0)
    spatial_bias = jnp.clip(jax.random.uniform(seeds[8], (MID,), jnp.float32, -0.8, 0.8), -0.8, 0.8)
    expand_scale = jnp.clip(jnp.exp(jax.random.uniform(seeds[9], (CIN,), jnp.float32, math.log(0.5), math.log(2.0))), 0.5, 2.0)
    expand_bias = jnp.clip(jax.random.uniform(seeds[10], (CIN,), jnp.float32, -0.8, 0.8), -0.8, 0.8)
    return {"frames": frames, "cotangent": cotangent, "reduce_weight": reduce_weight, "spatial_weight": spatial_weight, "expand_weight": expand_weight, "reduce_scale": reduce_scale, "reduce_bias": reduce_bias, "spatial_scale": spatial_scale, "spatial_bias": spatial_bias, "expand_scale": expand_scale, "expand_bias": expand_bias}


def activate(values):
    return jax.nn.gelu(values, approximate=True)

def matmul(left, right):
    return jnp.dot(left, right, precision=lax.Precision.HIGHEST, preferred_element_type=jnp.float32)

def shift_time(frames):
    folded = CIN // 8
    blank = jnp.zeros((1, HW, folded), jnp.float32)
    ahead = jnp.concatenate([frames[1:, :, :folded], blank], axis=0)
    behind = jnp.concatenate([blank, frames[:-1, :, folded:2 * folded]], axis=0)
    return jnp.concatenate([ahead, behind, frames[:, :, 2 * folded:]], axis=2)

def build_patches(picture):
    padded = jnp.pad(picture, ((0, 0), (1, 1), (1, 1), (0, 0)))
    pieces = [padded[:, row_off:row_off + SIDE, col_off:col_off + SIDE, :] for row_off in range(3) for col_off in range(3)]
    joined = jnp.concatenate(pieces, axis=3)
    return joined.reshape(picture.shape[0] * SIDE * SIDE, 9 * picture.shape[3])

def reference(frames, cotangent, reduce_weight, spatial_weight, expand_weight, reduce_scale, reduce_bias, spatial_scale, spatial_bias, expand_scale, expand_bias):
    nframes = frames.shape[0]
    rowcount = nframes * HW

    def forward(inputs, first_weight, second_weight, third_weight):
        shifted = shift_time(inputs).reshape(rowcount, CIN)
        hidden_one = activate(reduce_scale * matmul(shifted, first_weight) + reduce_bias)
        patches = build_patches(hidden_one.reshape(nframes, SIDE, SIDE, MID))
        hidden_two = activate(spatial_scale * matmul(patches, second_weight) + spatial_bias)
        pre_out = expand_scale * matmul(hidden_two, third_weight.T) + expand_bias + inputs.reshape(rowcount, CIN)
        return activate(pre_out).reshape(nframes, HW, CIN)
    block_out, backward = jax.vjp(forward, frames, reduce_weight, spatial_weight, expand_weight)
    grad_frames, grad_reduce, grad_spatial, grad_expand = backward(cotangent)
    return (block_out, grad_frames, grad_reduce, grad_spatial, grad_expand)
```

```python
import functools
import math

import jax
import jax.numpy as jnp
from jax import lax
from jax.experimental import pallas as pl
from jax.experimental.pallas import tpu as pltpu
from jax.sharding import PartitionSpec as P

F32 = jnp.float32
BF16 = jnp.bfloat16
ROOT = math.sqrt(2.0 / math.pi)
CUBE = 0.044715
NN = (((1,), (0,)), ((), ()))
NT = (((1,), (1,)), ((), ()))


def passed_along(block, axis, distance):
    devices = range(lax.axis_size(axis))
    route = [(i - distance, i) for i in devices if i - distance in devices]
    return lax.ppermute(block, axis, route)


def split(values):
    high = values.astype(BF16)
    low = (values - high.astype(F32)).astype(BF16)
    return high, low


def product(left, right, dims=NN):
    def one(a, b):
        return lax.dot_general(a, b, dims, preferred_element_type=F32)

    return one(left[0], right[0]) + (one(left[0], right[1]) + one(left[1], right[0]))


def gelu_pair(values):
    square = values * values
    turned = jnp.tanh(ROOT * values * (1.0 + CUBE * square))
    half = 0.5 * (1.0 + turned)
    slope = half + (0.5 * ROOT) * values * (1.0 - turned * turned) * (
        1.0 + (3.0 * CUBE) * square
    )
    return values * half, slope


def pick(pair, index):
    return pair[0][index], pair[1][index]


class Sizes:
    def __init__(self, nframes, ncells, channels, middle, shards):
        self.nframes, self.ncells = nframes, ncells
        self.channels, self.middle, self.shards = channels, middle, shards
        self.extent = math.isqrt(ncells)
        self.pitch = 16
        self.rows = self.extent * self.pitch
        self.tall = (self.extent + 2) * self.pitch
        self.folded = channels // 8


def to_pitch(sz, target, frame, flat):
    for row in range(sz.extent):
        at = 8 + sz.pitch * (row + 1)
        target[frame, at : at + sz.extent, :] = flat[row * sz.extent : (row + 1) * sz.extent]


def to_flat(sz, target, frame, pitched):
    for row in range(sz.extent):
        target[frame, row * sz.extent : (row + 1) * sz.extent, :] = pitched[
            row * sz.pitch : row * sz.pitch + sz.extent
        ]


def slot_source(sz, slot):
    bits = sz.shards.bit_length() - 1
    turned = sum(((slot >> (bits - 1 - b)) & 1) << b for b in range(bits))
    return turned


def write_slots(sz, me, source, outs):
    rows = source.shape[0] // sz.shards
    base = sz.shards
    for out in outs:
        count = out.shape[0] // rows
        base -= count
        for k in range(count):
            chunk = jnp.bitwise_xor(me, slot_source(sz, base + k))
            out[k * rows : (k + 1) * rows, :] = source[
                pl.ds(pl.multiple_of(chunk * rows, 8), rows), :
            ]


def slot_shapes(sz, total, width):
    rows = total // sz.shards
    counts, left = [], sz.shards
    while left > 1:
        left //= 2
        counts.append(left)
    counts.append(1)
    return [jax.ShapeDtypeStruct((c * rows, width), F32) for c in counts]


def begin_kernel(sz, frames, weight, part):
    f = sz.folded
    w = split(weight[...])
    for t in range(sz.nframes):
        total = product(split(frames[t, :, 2 * f :]), pick(w, slice(2 * f, None)))
        if t + 1 < sz.nframes:
            total += product(split(frames[t + 1, :, :f]), pick(w, slice(0, f)))
        if t > 0:
            total += product(split(frames[t - 1, :, f : 2 * f]), pick(w, slice(f, 2 * f)))
        part[t] = total


def middle_kernel(
    sz, naturals, me_ref, part, from_next, from_prev, frames, cotangent, w1, w2, w3,
    rs, rb, ss, sb, es, eb, *refs
):
    block_out, residual, padded_one, padded_grad, slope_one = refs[:5]
    outs, (high, low, flat, whole) = refs[5:-4], refs[-4:]
    f, n = sz.folded, sz.nframes
    padded_one[...] = jnp.zeros_like(padded_one)
    padded_grad[...] = jnp.zeros_like(padded_grad)
    for t in range(n):
        pre = part[t]
        if t + 1 == n:
            pre += product(split(from_next[0]), split(w1[:f, :]))
        if t == 0:
            pre += product(split(from_prev[0]), split(w1[f : 2 * f, :]))
        hidden, slope = gelu_pair(rs[...] * pre + rb[...])
        slope_one[t] = slope * rs[...]
        to_pitch(sz, padded_one, t, hidden)
    for c in range(3):
        h, l = split(padded_one[:, 7 + c : 7 + c + sz.tall, :])
        high[c], low[c] = h, l
    total = jnp.zeros((n * sz.rows, sz.middle), F32)
    for r in range(3):
        for c in range(3):
            tap = 3 * r + c
            cut = slice(sz.pitch * r, sz.pitch * r + sz.rows)
            left = (
                high[c, :, cut, :].reshape(n * sz.rows, sz.middle),
                low[c, :, cut, :].reshape(n * sz.rows, sz.middle),
            )
            total += product(left, split(w2[tap * sz.middle : (tap + 1) * sz.middle, :]))
    hidden_two, slope_two = gelu_pair(ss[...] * total + sb[...])
    slope_two = slope_two * ss[...]
    w = split(w3[...])
    for t in range(n):
        to_flat(sz, flat, t, hidden_two[t * sz.rows : (t + 1) * sz.rows])
    for t in range(n):
        pre = es[...] * product(split(flat[t]), w, NT) + eb[...] + frames[t]
        block, slope = gelu_pair(pre)
        block_out[t] = block
        residual[t] = cotangent[t] * slope
    total = [None] * n
    for t in range(n):
        grad = residual[t] * es[...]
        back = product(split(grad), w)
        for row in range(sz.extent):
            at = 8 + sz.pitch * (row + 1)
            lo = t * sz.rows + row * sz.pitch
            padded_grad[t, at : at + sz.extent, :] = (
                back[row * sz.extent : (row + 1) * sz.extent]
                * slope_two[lo : lo + sz.extent]
            )
    step = 256
    for lo in range(0, sz.channels, step):
        total = jnp.zeros((step, sz.middle), F32)
        for t in range(n):
            grad = residual[t, :, lo : lo + step] * es[:, lo : lo + step]
            total += product(split(grad.T), split(flat[t]))
        whole[lo : lo + step, :] = total
    if naturals:
        outs[0][...] = whole[...]
    else:
        write_slots(sz, me_ref[0], whole, outs)


def shifted_grads(sz, padded_grad, c):
    return split(padded_grad[:, 9 - c : 9 - c + sz.tall, :])


def spatial_kernel(sz, naturals, me_ref, padded_one, padded_grad, *refs):
    outs, (whole,) = refs[:-1], refs[-1:]
    n = sz.nframes
    at = 8 + sz.pitch
    turned = split(
        padded_one[:, at : at + sz.rows, :].reshape(n * sz.rows, sz.middle).T
    )
    for c in range(3):
        pair = shifted_grads(sz, padded_grad, c)
        for r in range(3):
            tap = 3 * r + c
            cut = slice(sz.pitch * (2 - r), sz.pitch * (2 - r) + sz.rows)
            right = tuple(x[:, cut, :].reshape(n * sz.rows, sz.middle) for x in pair)
            whole[tap * sz.middle : (tap + 1) * sz.middle, :] = product(turned, right)
    if naturals:
        outs[0][...] = whole[...]
    else:
        write_slots(sz, me_ref[0], whole, outs)


def reduce_kernel(
    sz, naturals, me_ref, padded_grad, slope_one, w2, w1, frames, from_next, from_prev, *refs
):
    reduce_grad, ahead, behind = refs[:3]
    outs, (whole,) = refs[3:-1], refs[-1:]
    n, f = sz.nframes, sz.folded
    total = jnp.zeros((n * sz.rows, sz.middle), F32)
    for c in range(3):
        pair = shifted_grads(sz, padded_grad, c)
        for r in range(3):
            tap = 3 * r + c
            cut = slice(sz.pitch * (2 - r), sz.pitch * (2 - r) + sz.rows)
            left = tuple(x[:, cut, :].reshape(n * sz.rows, sz.middle) for x in pair)
            total += product(left, split(w2[tap * sz.middle : (tap + 1) * sz.middle, :]), NT)
    for t in range(n):
        for row in range(sz.extent):
            lo = t * sz.rows + row * sz.pitch
            cut = slice(row * sz.extent, (row + 1) * sz.extent)
            reduce_grad[t, cut, :] = total[lo : lo + sz.extent] * slope_one[t, cut, :]
    ahead[0] = product(split(reduce_grad[n - 1]), split(w1[:f, :]), NT)
    behind[0] = product(split(reduce_grad[0]), split(w1[f : 2 * f, :]), NT)
    pairs = [split(reduce_grad[t]) for t in range(n)]
    for lo in range(0, sz.channels, f):
        total = jnp.zeros((f, sz.middle), F32)
        for t in range(n):
            if lo == 0:
                block = frames[t + 1, :, :f] if t + 1 < n else from_next[0]
            elif lo == f:
                block = frames[t - 1, :, f : 2 * f] if t > 0 else from_prev[0]
            else:
                block = frames[t, :, lo : lo + f]
            total += product(split(block.T), pairs[t])
        whole[lo : lo + f, :] = total
    if naturals:
        outs[0][...] = whole[...]
    else:
        write_slots(sz, me_ref[0], whole, outs)


def end_kernel(sz, reduce_grad, w1, residual, before, after, grad_frames):
    n, f = sz.nframes, sz.folded
    w = split(w1[...])
    for t in range(n):
        back = product(split(reduce_grad[t]), w, NT)
        grad_frames[t, :, 2 * f :] = residual[t, :, 2 * f :] + back[:, 2 * f :]
        if t + 1 < n:
            grad_frames[t + 1, :, :f] = residual[t + 1, :, :f] + back[:, :f]
        if t > 0:
            grad_frames[t - 1, :, f : 2 * f] = (
                residual[t - 1, :, f : 2 * f] + back[:, f : 2 * f]
            )
    grad_frames[0, :, :f] = residual[0, :, :f] + before[0]
    grad_frames[n - 1, :, f : 2 * f] = residual[n - 1, :, f : 2 * f] + after[0]


VM = pl.BlockSpec(memory_space=pltpu.VMEM)
SM = pl.BlockSpec(memory_space=pltpu.SMEM)


def call(kernel, outs, ins, scratch=(), scalar=False, flops=0, name=None):
    specs = [VM] * len(ins)
    if scalar:
        specs[0] = SM
    moved = sum(4 * math.prod(x.shape) for x in list(ins) + list(outs))
    return pl.pallas_call(
        kernel,
        out_shape=list(outs),
        in_specs=specs,
        out_specs=[VM] * len(outs),
        scratch_shapes=list(scratch),
        compiler_params=pltpu.CompilerParams(vmem_limit_bytes=60000 * 1024),
        cost_estimate=pl.CostEstimate(flops=flops, bytes_accessed=moved, transcendentals=0),
        name=name,
    )(*ins)


def scatter_sum(sz, pieces):
    shards = sz.shards
    if len(pieces) == 1:
        return lax.psum_scatter(pieces[0], "tm", scatter_dimension=0, tiled=True)
    distance, arrived = 1, []
    for piece in pieces[:-1]:
        rows = piece.shape[0]
        for block in arrived:
            piece = piece + block[rows : 2 * rows]
        arrived.append(
            lax.ppermute(piece, "tm", [(i, i ^ distance) for i in range(shards)])
        )
        distance *= 2
    total = pieces[-1]
    for block in arrived:
        total = total + block[: total.shape[0]]
    return total


def local(
    frames,
    cotangent,
    reduce_weight,
    spatial_weight,
    expand_weight,
    reduce_scale,
    reduce_bias,
    spatial_scale,
    spatial_bias,
    expand_scale,
    expand_bias,
):
    nframes, ncells, channels = frames.shape
    middle = reduce_weight.shape[1]
    shards = lax.axis_size("tm")
    sz = Sizes(nframes, ncells, channels, middle, shards)
    f = sz.folded
    power = shards & (shards - 1) == 0

    def natural(total):
        return not (power and shards > 1 and total % (8 * shards) == 0)

    def grads(total):
        if natural(total):
            return [jax.ShapeDtypeStruct((total, middle), F32)]
        return slot_shapes(sz, total, middle)

    def full(*shape):
        return jax.ShapeDtypeStruct(shape, F32)

    me = lax.axis_index("tm").astype(jnp.int32).reshape(1)
    work = 6 * nframes * ncells * middle
    from_next = passed_along(frames[:1, :, :f], "tm", -1)
    from_prev = passed_along(frames[-1:, :, f : 2 * f], "tm", 1)
    vectors = [
        x.reshape(1, -1)
        for x in (reduce_scale, reduce_bias, spatial_scale, spatial_bias, expand_scale, expand_bias)
    ]
    (part,) = call(
        functools.partial(begin_kernel, sz),
        [full(nframes, ncells, middle)],
        [frames, reduce_weight],
        flops=work * channels,
        name="begin",
    )
    block_out, residual, padded_one, padded_grad, slope_one, *expand_pieces = call(
        functools.partial(middle_kernel, sz, natural(channels)),
        [
            full(nframes, ncells, channels),
            full(nframes, ncells, channels),
            full(nframes, sz.tall + 16, middle),
            full(nframes, sz.tall + 16, middle),
            full(nframes, ncells, middle),
        ]
        + grads(channels),
        [me, part, from_next, from_prev, frames, cotangent, reduce_weight, spatial_weight,
         expand_weight] + vectors,
        [
            pltpu.VMEM((3, nframes, sz.tall, middle), BF16),
            pltpu.VMEM((3, nframes, sz.tall, middle), BF16),
            pltpu.VMEM((nframes, ncells, middle), F32),
            pltpu.VMEM((channels, middle), F32),
        ],
        scalar=True,
        flops=work * (9 * middle + 3 * channels),
        name="middle",
    )
    grad_expand = scatter_sum(sz, expand_pieces)
    spatial_pieces = call(
        functools.partial(spatial_kernel, sz, natural(9 * middle)),
        grads(9 * middle),
        [me, padded_one, padded_grad],
        [pltpu.VMEM((9 * middle, middle), F32)],
        scalar=True,
        flops=work * 9 * middle,
        name="spatial",
    )
    grad_spatial = scatter_sum(sz, spatial_pieces)
    reduce_grad, ahead, behind, *reduce_pieces = call(
        functools.partial(reduce_kernel, sz, natural(channels)),
        [full(nframes, ncells, middle), full(1, ncells, f), full(1, ncells, f)] + grads(channels),
        [me, padded_grad, slope_one, spatial_weight, reduce_weight, frames, from_next, from_prev],
        [pltpu.VMEM((channels, middle), F32)],
        scalar=True,
        flops=work * (9 * middle + channels),
        name="reduce",
    )
    before = passed_along(ahead, "tm", 1)
    after = passed_along(behind, "tm", -1)
    grad_reduce = scatter_sum(sz, reduce_pieces)
    (grad_frames,) = call(
        functools.partial(end_kernel, sz),
        [full(nframes, ncells, channels)],
        [reduce_grad, reduce_weight, residual, before, after],
        flops=work * channels,
        name="end",
    )
    return block_out, grad_frames, grad_reduce, grad_spatial, grad_expand


def solution(mesh):
    return jax.shard_map(
        local,
        mesh=mesh,
        in_specs=(
            P(("groups", "tm"), None, None),
            P(("groups", "tm"), None, None),
            P(),
            P(),
            P(),
            P(),
            P(),
            P(),
            P(),
            P(),
            P(),
        ),
        out_specs=(
            P(("groups", "tm"), None, None),
            P(("groups", "tm"), None, None),
            P(("groups", "tm"), None),
            P(("groups", "tm"), None),
            P(("groups", "tm"), None),
        ),
        check_vma=False,
    )
```

```python
import functools
import math

import jax
import jax.numpy as jnp
from jax import lax
from jax.experimental import pallas as pl
from jax.experimental.pallas import tpu as pltpu
from jax.sharding import PartitionSpec as P


F32 = jnp.float32
BF16 = jnp.bfloat16
ROOT = math.sqrt(2.0 / math.pi)
CUBE = 0.044715
NN = (((1,), (0,)), ((), ()))
NT = (((1,), (1,)), ((), ()))


def passed_along(block, axis, distance):
    devices = range(lax.axis_size(axis))
    route = [(i - distance, i) for i in devices if i - distance in devices]
    return lax.ppermute(block, axis, route)


def split(values):
    high = values.astype(BF16)
    low = (values - high.astype(F32)).astype(BF16)
    return high, low


def product(left, right, dims=NN):
    def one(a, b):
        return lax.dot_general(a, b, dims, preferred_element_type=F32)

    return one(left[0], right[0]) + (one(left[0], right[1]) + one(left[1], right[0]))


def gelu_pair(values):
    square = values * values
    turned = jnp.tanh(ROOT * values * (1.0 + CUBE * square))
    half = 0.5 * (1.0 + turned)
    slope = half + (0.5 * ROOT) * values * (1.0 - turned * turned) * (
        1.0 + (3.0 * CUBE) * square
    )
    return values * half, slope


def pick(pair, index):
    return pair[0][index], pair[1][index]


class Sizes:
    def __init__(self, nframes, ncells, channels, middle, shards):
        self.nframes, self.ncells = nframes, ncells
        self.channels, self.middle, self.shards = channels, middle, shards
        self.extent = math.isqrt(ncells)
        self.pitch = 16
        self.rows = self.extent * self.pitch
        self.tall = (self.extent + 2) * self.pitch
        self.folded = channels // 8


def view(array):
    nframes, ncells, channels = array.shape
    turned = array.transpose(1, 0, 2).reshape(ncells, nframes, channels // 128, 128)
    return turned.transpose(0, 2, 1, 3).reshape(-1, 128)


def unview(rows, shape):
    nframes, ncells, channels = shape
    turned = rows.reshape(ncells, channels // 128, nframes, 128).transpose(0, 2, 1, 3)
    return turned.reshape(ncells, nframes, channels).transpose(1, 0, 2)


def tile_rows(sz, t, tile):
    return pl.ds(sz.nframes * tile + t, sz.ncells, stride=sz.nframes * (sz.channels // 128))


def take(sz, ref, t, lo=0, hi=None):
    hi = sz.channels if hi is None else hi
    tiles = [ref[tile_rows(sz, t, j), :] for j in range(lo // 128, hi // 128)]
    return tiles[0] if len(tiles) == 1 else jnp.concatenate(tiles, axis=1)


def put(sz, ref, t, values, lo=0):
    for j in range(values.shape[1] // 128):
        ref[tile_rows(sz, t, lo // 128 + j), :] = values[:, 128 * j : 128 * (j + 1)]


def to_pitch(sz, target, frame, flat):
    for row in range(sz.extent):
        at = 8 + sz.pitch * (row + 1)
        target[frame, at : at + sz.extent, :] = flat[row * sz.extent : (row + 1) * sz.extent]


def to_flat(sz, target, frame, pitched):
    for row in range(sz.extent):
        target[frame, row * sz.extent : (row + 1) * sz.extent, :] = pitched[
            row * sz.pitch : row * sz.pitch + sz.extent
        ]


def slot_source(slot, order):
    bits = len(order)
    return sum(((slot >> (bits - 1 - b)) & 1) * order[b] for b in range(bits))


def write_slots(sz, me, source, outs, order):
    rows = source.shape[0] // sz.shards
    base = sz.shards
    for out in outs:
        count = out.shape[0] // rows
        base -= count
        for k in range(count):
            chunk = jnp.bitwise_xor(me, slot_source(base + k, order))
            out[k * rows : (k + 1) * rows, :] = source[
                pl.ds(pl.multiple_of(chunk * rows, 8), rows), :
            ]


def slot_shapes(sz, total, width):
    rows = total // sz.shards
    counts, left = [], sz.shards
    while left > 1:
        left //= 2
        counts.append(left)
    counts.append(1)
    return [jax.ShapeDtypeStruct((c * rows, width), F32) for c in counts]


def begin_kernel(sz, frames, weight, part):
    f = sz.folded
    w = split(weight[...])
    for t in range(sz.nframes):
        total = product(split(take(sz, frames, t, 2 * f)), pick(w, slice(2 * f, None)))
        if t + 1 < sz.nframes:
            total += product(split(take(sz, frames, t + 1, 0, f)), pick(w, slice(0, f)))
        if t > 0:
            total += product(split(take(sz, frames, t - 1, f, 2 * f)), pick(w, slice(f, 2 * f)))
        part[t] = total


def middle_kernel(
    sz, part, from_next, from_prev, frames, cotangent, w1, w2, w3,
    rs, rb, ss, sb, es, eb, *refs
):
    block_out, residual, padded_one, padded_grad, slope_one, flat, high, low = refs
    f, n = sz.folded, sz.nframes
    padded_one[...] = jnp.zeros_like(padded_one)
    padded_grad[...] = jnp.zeros_like(padded_grad)
    for t in range(n):
        pre = part[t]
        if t + 1 == n:
            pre += product(split(from_next[0]), split(w1[:f, :]))
        if t == 0:
            pre += product(split(from_prev[0]), split(w1[f : 2 * f, :]))
        hidden, slope = gelu_pair(rs[...] * pre + rb[...])
        slope_one[t] = slope * rs[...]
        to_pitch(sz, padded_one, t, hidden)
    for c in range(3):
        h, l = split(padded_one[:, 7 + c : 7 + c + sz.tall, :])
        high[c], low[c] = h, l
    total = jnp.zeros((n * sz.rows, sz.middle), F32)
    for r in range(3):
        for c in range(3):
            tap = 3 * r + c
            cut = slice(sz.pitch * r, sz.pitch * r + sz.rows)
            left = (
                high[c, :, cut, :].reshape(n * sz.rows, sz.middle),
                low[c, :, cut, :].reshape(n * sz.rows, sz.middle),
            )
            total += product(left, split(w2[tap * sz.middle : (tap + 1) * sz.middle, :]))
    hidden_two, slope_two = gelu_pair(ss[...] * total + sb[...])
    slope_two = slope_two * ss[...]
    w = split(w3[...])
    for t in range(n):
        to_flat(sz, flat, t, hidden_two[t * sz.rows : (t + 1) * sz.rows])
    for t in range(n):
        pre = es[...] * product(split(flat[t]), w, NT) + eb[...] + take(sz, frames, t)
        block, slope = gelu_pair(pre)
        put(sz, block_out, t, block)
        residual[t] = take(sz, cotangent, t) * slope
    for t in range(n):
        grad = residual[t] * es[...]
        back = product(split(grad), w)
        for row in range(sz.extent):
            at = 8 + sz.pitch * (row + 1)
            lo = t * sz.rows + row * sz.pitch
            padded_grad[t, at : at + sz.extent, :] = (
                back[row * sz.extent : (row + 1) * sz.extent]
                * slope_two[lo : lo + sz.extent]
            )


def expand_kernel(sz, order, me_ref, residual, flat, es, *refs):
    outs, (whole,) = refs[:-1], refs[-1:]
    pairs = [split(flat[t]) for t in range(sz.nframes)]
    step = 256
    for lo in range(0, sz.channels, step):
        total = jnp.zeros((step, sz.middle), F32)
        for t in range(sz.nframes):
            grad = residual[t, :, lo : lo + step] * es[:, lo : lo + step]
            total += product(split(grad.T), pairs[t])
        whole[lo : lo + step, :] = total
    if order is None:
        outs[0][...] = whole[...]
    else:
        write_slots(sz, me_ref[0], whole, outs, order)


def shifted_grads(sz, padded_grad, c):
    return split(padded_grad[:, 9 - c : 9 - c + sz.tall, :])


def spatial_kernel(sz, order, me_ref, padded_one, padded_grad, *refs):
    outs, (whole,) = refs[:-1], refs[-1:]
    n = sz.nframes
    at = 8 + sz.pitch
    turned = split(
        padded_one[:, at : at + sz.rows, :].reshape(n * sz.rows, sz.middle).T
    )
    for c in range(3):
        pair = shifted_grads(sz, padded_grad, c)
        for r in range(3):
            tap = 3 * r + c
            cut = slice(sz.pitch * (2 - r), sz.pitch * (2 - r) + sz.rows)
            right = tuple(x[:, cut, :].reshape(n * sz.rows, sz.middle) for x in pair)
            whole[tap * sz.middle : (tap + 1) * sz.middle, :] = product(turned, right)
    if order is None:
        outs[0][...] = whole[...]
    else:
        write_slots(sz, me_ref[0], whole, outs, order)


def reduce_kernel(
    sz, order, me_ref, padded_grad, slope_one, w2, w1, frames, from_next, from_prev, *refs
):
    reduce_grad, ahead, behind = refs[:3]
    outs, (whole,) = refs[3:-1], refs[-1:]
    n, f = sz.nframes, sz.folded
    total = jnp.zeros((n * sz.rows, sz.middle), F32)
    for c in range(3):
        pair = shifted_grads(sz, padded_grad, c)
        for r in range(3):
            tap = 3 * r + c
            cut = slice(sz.pitch * (2 - r), sz.pitch * (2 - r) + sz.rows)
            left = tuple(x[:, cut, :].reshape(n * sz.rows, sz.middle) for x in pair)
            total += product(left, split(w2[tap * sz.middle : (tap + 1) * sz.middle, :]), NT)
    for t in range(n):
        for row in range(sz.extent):
            lo = t * sz.rows + row * sz.pitch
            cut = slice(row * sz.extent, (row + 1) * sz.extent)
            reduce_grad[t, cut, :] = total[lo : lo + sz.extent] * slope_one[t, cut, :]
    ahead[0] = product(split(reduce_grad[n - 1]), split(w1[:f, :]), NT)
    behind[0] = product(split(reduce_grad[0]), split(w1[f : 2 * f, :]), NT)
    pairs = [split(reduce_grad[t]) for t in range(n)]
    for lo in range(0, sz.channels, f):
        total = jnp.zeros((f, sz.middle), F32)
        for t in range(n):
            if lo == 0:
                block = take(sz, frames, t + 1, 0, f) if t + 1 < n else from_next[0]
            elif lo == f:
                block = take(sz, frames, t - 1, f, 2 * f) if t > 0 else from_prev[0]
            else:
                block = take(sz, frames, t, lo, lo + f)
            total += product(split(block.T), pairs[t])
        whole[lo : lo + f, :] = total
    if order is None:
        outs[0][...] = whole[...]
    else:
        write_slots(sz, me_ref[0], whole, outs, order)


def end_kernel(sz, reduce_grad, w1, residual, before, after, grad_frames):
    n, f = sz.nframes, sz.folded
    w = split(w1[...])
    for t in range(n):
        back = product(split(reduce_grad[t]), w, NT)
        put(sz, grad_frames, t, residual[t, :, 2 * f :] + back[:, 2 * f :], 2 * f)
        if t + 1 < n:
            put(sz, grad_frames, t + 1, residual[t + 1, :, :f] + back[:, :f])
        if t > 0:
            put(
                sz, grad_frames, t - 1,
                residual[t - 1, :, f : 2 * f] + back[:, f : 2 * f], f,
            )
    put(sz, grad_frames, 0, residual[0, :, :f] + before[0])
    put(sz, grad_frames, n - 1, residual[n - 1, :, f : 2 * f] + after[0], f)


VM = pl.BlockSpec(memory_space=pltpu.VMEM)
SM = pl.BlockSpec(memory_space=pltpu.SMEM)


def call(kernel, outs, ins, scratch=(), scalar=False, flops=0):
    specs = [VM] * len(ins)
    if scalar:
        specs[0] = SM
    moved = sum(4 * math.prod(x.shape) for x in list(ins) + list(outs))
    return pl.pallas_call(
        kernel,
        out_shape=list(outs),
        in_specs=specs,
        out_specs=[VM] * len(outs),
        scratch_shapes=list(scratch),
        compiler_params=pltpu.CompilerParams(vmem_limit_bytes=58 * 1024 * 1024),
        cost_estimate=pl.CostEstimate(flops=flops, bytes_accessed=moved, transcendentals=0),
    )(*ins)


def scatter_sum(sz, pieces, order):
    shards = sz.shards
    if order is None:
        return lax.psum_scatter(pieces[0], "tm", scatter_dimension=0, tiled=True)
    arrived = []
    for stage, piece in enumerate(pieces[:-1]):
        rows = piece.shape[0]
        for block in arrived:
            piece = piece + block[rows : 2 * rows]
        route = [(i, i ^ order[stage]) for i in range(shards)]
        arrived.append(lax.ppermute(piece, "tm", route))
    total = pieces[-1]
    for block in arrived:
        total = total + block[: total.shape[0]]
    return total


def local(
    frames,
    cotangent,
    reduce_weight,
    spatial_weight,
    expand_weight,
    reduce_scale,
    reduce_bias,
    spatial_scale,
    spatial_bias,
    expand_scale,
    expand_bias,
):
    nframes, ncells, channels = frames.shape
    middle = reduce_weight.shape[1]
    shards = lax.axis_size("tm")
    sz = Sizes(nframes, ncells, channels, middle, shards)
    f = sz.folded

    def order_of(total):
        if shards & (shards - 1) or shards == 1 or total % (8 * shards):
            return None
        return [1 << b for b in range(shards.bit_length() - 1)]

    def grads(total):
        if order_of(total) is None:
            return [jax.ShapeDtypeStruct((total, middle), F32)]
        return slot_shapes(sz, total, middle)

    def full(*shape):
        return jax.ShapeDtypeStruct(shape, F32)

    me = lax.axis_index("tm").astype(jnp.int32).reshape(1)
    work = 6 * nframes * ncells * middle
    from_next = passed_along(frames[:1, :, :f], "tm", -1)
    from_prev = passed_along(frames[-1:, :, f : 2 * f], "tm", 1)
    rs, rb, ss, sb, es, eb = [
        x.reshape(1, -1)
        for x in (reduce_scale, reduce_bias, spatial_scale, spatial_bias, expand_scale, expand_bias)
    ]
    frame_rows = view(frames)
    lines = full(*frame_rows.shape)
    (part,) = call(
        functools.partial(begin_kernel, sz),
        [full(nframes, ncells, middle)],
        [frame_rows, reduce_weight],
        flops=work * channels,
    )
    block_out, residual, padded_one, padded_grad, slope_one, flat = call(
        functools.partial(middle_kernel, sz),
        [
            lines,
            full(nframes, ncells, channels),
            full(nframes, sz.tall + 16, middle),
            full(nframes, sz.tall + 16, middle),
            full(nframes, ncells, middle),
            full(nframes, ncells, middle),
        ],
        [part, from_next, from_prev, frame_rows, view(cotangent), reduce_weight, spatial_weight,
         expand_weight, rs, rb, ss, sb, es, eb],
        [
            pltpu.VMEM((3, nframes, sz.tall, middle), BF16),
            pltpu.VMEM((3, nframes, sz.tall, middle), BF16),
        ],
        flops=work * (9 * middle + 2 * channels),
    )
    spatial_order, channel_order = order_of(9 * middle), order_of(channels)
    spatial_pieces = call(
        functools.partial(spatial_kernel, sz, spatial_order),
        grads(9 * middle),
        [me, padded_one, padded_grad],
        [pltpu.VMEM((9 * middle, middle), F32)],
        scalar=True,
        flops=work * 9 * middle,
    )
    grad_spatial = scatter_sum(sz, spatial_pieces, spatial_order)
    expand_pieces = call(
        functools.partial(expand_kernel, sz, channel_order),
        grads(channels),
        [me, residual, flat, es],
        [pltpu.VMEM((channels, middle), F32)],
        scalar=True,
        flops=work * channels,
    )
    grad_expand = scatter_sum(sz, expand_pieces, channel_order)
    reduce_grad, ahead, behind, *reduce_pieces = call(
        functools.partial(reduce_kernel, sz, channel_order),
        [full(nframes, ncells, middle), full(1, ncells, f), full(1, ncells, f)] + grads(channels),
        [me, padded_grad, slope_one, spatial_weight, reduce_weight, frame_rows, from_next, from_prev],
        [pltpu.VMEM((channels, middle), F32)],
        scalar=True,
        flops=work * (9 * middle + channels),
    )
    before = passed_along(ahead, "tm", 1)
    after = passed_along(behind, "tm", -1)
    grad_reduce = scatter_sum(sz, reduce_pieces, channel_order)
    (grad_frames,) = call(
        functools.partial(end_kernel, sz),
        [lines],
        [reduce_grad, reduce_weight, residual, before, after],
        flops=work * channels,
    )
    return (
        unview(block_out, frames.shape),
        unview(grad_frames, frames.shape),
        grad_reduce,
        grad_spatial,
        grad_expand,
    )


def solution(mesh):
    return jax.shard_map(
        local,
        mesh=mesh,
        in_specs=(
            P(("groups", "tm"), None, None),
            P(("groups", "tm"), None, None),
            P(),
            P(),
            P(),
            P(),
            P(),
            P(),
            P(),
            P(),
            P(),
        ),
        out_specs=(
            P(("groups", "tm"), None, None),
            P(("groups", "tm"), None, None),
            P(("groups", "tm"), None),
            P(("groups", "tm"), None),
            P(("groups", "tm"), None),
        ),
        check_vma=False,
    )
```

```python
import functools
import math

import jax
import jax.numpy as jnp
from jax import lax
from jax.experimental import pallas as pl
from jax.experimental.pallas import tpu as pltpu
from jax.sharding import PartitionSpec as P


F32 = jnp.float32
BF16 = jnp.bfloat16
ROOT = math.sqrt(2.0 / math.pi)
CUBE = 0.044715
NN = (((1,), (0,)), ((), ()))
NT = (((1,), (1,)), ((), ()))


def passed_along(block, axis, distance):
    devices = range(lax.axis_size(axis))
    route = [(i - distance, i) for i in devices if i - distance in devices]
    return lax.ppermute(block, axis, route)


def split(values):
    high = values.astype(BF16)
    low = (values - high.astype(F32)).astype(BF16)
    return high, low


def product(left, right, dims=NN):
    def one(a, b):
        return lax.dot_general(a, b, dims, preferred_element_type=F32)

    return one(left[0], right[0]) + (one(left[0], right[1]) + one(left[1], right[0]))


def gelu_pair(values):
    square = values * values
    turned = jnp.tanh(ROOT * values * (1.0 + CUBE * square))
    half = 0.5 * (1.0 + turned)
    slope = half + (0.5 * ROOT) * values * (1.0 - turned * turned) * (
        1.0 + (3.0 * CUBE) * square
    )
    return values * half, slope


def pick(pair, index):
    return pair[0][index], pair[1][index]


class Sizes:
    def __init__(self, nframes, ncells, channels, middle, shards):
        self.nframes, self.ncells = nframes, ncells
        self.channels, self.middle, self.shards = channels, middle, shards
        self.extent = math.isqrt(ncells)
        self.pitch = 16
        self.rows = self.extent * self.pitch
        self.tall = (self.extent + 2) * self.pitch
        self.folded = channels // 8


def view(array):
    nframes, ncells, channels = array.shape
    turned = array.transpose(1, 0, 2).reshape(ncells, nframes, channels // 128, 128)
    return turned.transpose(0, 2, 1, 3).reshape(-1, 128)


def unview(rows, shape):
    nframes, ncells, channels = shape
    turned = rows.reshape(ncells, channels // 128, nframes, 128).transpose(0, 2, 1, 3)
    return turned.reshape(ncells, nframes, channels).transpose(1, 0, 2)


def tile_rows(sz, t, tile):
    return pl.ds(sz.nframes * tile + t, sz.ncells, stride=sz.nframes * (sz.channels // 128))


def take(sz, ref, t, lo=0, hi=None):
    hi = sz.channels if hi is None else hi
    tiles = [ref[tile_rows(sz, t, j), :] for j in range(lo // 128, hi // 128)]
    return tiles[0] if len(tiles) == 1 else jnp.concatenate(tiles, axis=1)


def put(sz, ref, t, values, lo=0):
    for j in range(values.shape[1] // 128):
        ref[tile_rows(sz, t, lo // 128 + j), :] = values[:, 128 * j : 128 * (j + 1)]


def to_pitch(sz, target, frame, flat):
    for row in range(sz.extent):
        at = 8 + sz.pitch * (row + 1)
        target[frame, at : at + sz.extent, :] = flat[row * sz.extent : (row + 1) * sz.extent]


def to_flat(sz, target, frame, pitched):
    for row in range(sz.extent):
        target[frame, row * sz.extent : (row + 1) * sz.extent, :] = pitched[
            row * sz.pitch : row * sz.pitch + sz.extent
        ]


def slot_source(slot, order):
    bits = len(order)
    return sum(((slot >> (bits - 1 - b)) & 1) * order[b] for b in range(bits))


def write_slots(sz, me, source, outs, order):
    rows = source.shape[0] // sz.shards
    base = sz.shards
    for out in outs:
        count = out.shape[0] // rows
        base -= count
        for k in range(count):
            chunk = jnp.bitwise_xor(me, slot_source(base + k, order))
            out[k * rows : (k + 1) * rows, :] = source[
                pl.ds(pl.multiple_of(chunk * rows, 8), rows), :
            ]


def slot_shapes(sz, total, width):
    rows = total // sz.shards
    counts, left = [], sz.shards
    while left > 1:
        left //= 2
        counts.append(left)
    counts.append(1)
    return [jax.ShapeDtypeStruct((c * rows, width), F32) for c in counts]


def begin_kernel(sz, frames, weight, part):
    f = sz.folded
    w = split(weight[...])
    for t in range(sz.nframes):
        total = product(split(take(sz, frames, t, 2 * f)), pick(w, slice(2 * f, None)))
        if t + 1 < sz.nframes:
            total += product(split(take(sz, frames, t + 1, 0, f)), pick(w, slice(0, f)))
        if t > 0:
            total += product(split(take(sz, frames, t - 1, f, 2 * f)), pick(w, slice(f, 2 * f)))
        part[t] = total


def middle_kernel(
    sz, part, from_next, from_prev, frames, cotangent, w1, w2, w3,
    rs, rb, ss, sb, es, eb, *refs
):
    block_out, residual, padded_one, padded_grad, slope_one, flat, high, low = refs
    f, n = sz.folded, sz.nframes
    padded_one[...] = jnp.zeros_like(padded_one)
    padded_grad[...] = jnp.zeros_like(padded_grad)
    for t in range(n):
        pre = part[t]
        if t + 1 == n:
            pre += product(split(from_next[0]), split(w1[:f, :]))
        if t == 0:
            pre += product(split(from_prev[0]), split(w1[f : 2 * f, :]))
        hidden, slope = gelu_pair(rs[...] * pre + rb[...])
        slope_one[t] = slope * rs[...]
        to_pitch(sz, padded_one, t, hidden)
    for c in range(3):
        h, l = split(padded_one[:, 7 + c : 7 + c + sz.tall, :])
        high[c], low[c] = h, l
    total = jnp.zeros((n * sz.rows, sz.middle), F32)
    for r in range(3):
        for c in range(3):
            tap = 3 * r + c
            cut = slice(sz.pitch * r, sz.pitch * r + sz.rows)
            left = (
                high[c, :, cut, :].reshape(n * sz.rows, sz.middle),
                low[c, :, cut, :].reshape(n * sz.rows, sz.middle),
            )
            total += product(left, split(w2[tap * sz.middle : (tap + 1) * sz.middle, :]))
    hidden_two, slope_two = gelu_pair(ss[...] * total + sb[...])
    slope_two = slope_two * ss[...]
    w = split(w3[...])
    for t in range(n):
        to_flat(sz, flat, t, hidden_two[t * sz.rows : (t + 1) * sz.rows])
    for t in range(n):
        pre = es[...] * product(split(flat[t]), w, NT) + eb[...] + take(sz, frames, t)
        block, slope = gelu_pair(pre)
        put(sz, block_out, t, block)
        residual[t] = take(sz, cotangent, t) * slope
    for t in range(n):
        grad = residual[t] * es[...]
        back = product(split(grad), w)
        for row in range(sz.extent):
            at = 8 + sz.pitch * (row + 1)
            lo = t * sz.rows + row * sz.pitch
            padded_grad[t, at : at + sz.extent, :] = (
                back[row * sz.extent : (row + 1) * sz.extent]
                * slope_two[lo : lo + sz.extent]
            )


def expand_kernel(sz, order, me_ref, residual, flat, es, *refs):
    outs, (whole,) = refs[:-1], refs[-1:]
    pairs = [split(flat[t]) for t in range(sz.nframes)]
    step = 256
    for lo in range(0, sz.channels, step):
        total = jnp.zeros((step, sz.middle), F32)
        for t in range(sz.nframes):
            grad = residual[t, :, lo : lo + step] * es[:, lo : lo + step]
            total += product(split(grad.T), pairs[t])
        whole[lo : lo + step, :] = total
    if order is None:
        outs[0][...] = whole[...]
    else:
        write_slots(sz, me_ref[0], whole, outs, order)


def shifted_grads(sz, padded_grad, c):
    return split(padded_grad[:, 9 - c : 9 - c + sz.tall, :])


def spatial_kernel(sz, order, me_ref, padded_one, padded_grad, *refs):
    outs, (whole,) = refs[:-1], refs[-1:]
    n = sz.nframes
    at = 8 + sz.pitch
    turned = split(
        padded_one[:, at : at + sz.rows, :].reshape(n * sz.rows, sz.middle).T
    )
    for c in range(3):
        pair = shifted_grads(sz, padded_grad, c)
        for r in range(3):
            tap = 3 * r + c
            cut = slice(sz.pitch * (2 - r), sz.pitch * (2 - r) + sz.rows)
            right = tuple(x[:, cut, :].reshape(n * sz.rows, sz.middle) for x in pair)
            whole[tap * sz.middle : (tap + 1) * sz.middle, :] = product(turned, right)
    if order is None:
        outs[0][...] = whole[...]
    else:
        write_slots(sz, me_ref[0], whole, outs, order)


def reduce_kernel(
    sz, order, me_ref, padded_grad, slope_one, w2, w1, frames, from_next, from_prev, *refs
):
    reduce_grad, ahead, behind = refs[:3]
    outs, (whole,) = refs[3:-1], refs[-1:]
    n, f = sz.nframes, sz.folded
    total = jnp.zeros((n * sz.rows, sz.middle), F32)
    for c in range(3):
        pair = shifted_grads(sz, padded_grad, c)
        for r in range(3):
            tap = 3 * r + c
            cut = slice(sz.pitch * (2 - r), sz.pitch * (2 - r) + sz.rows)
            left = tuple(x[:, cut, :].reshape(n * sz.rows, sz.middle) for x in pair)
            total += product(left, split(w2[tap * sz.middle : (tap + 1) * sz.middle, :]), NT)
    for t in range(n):
        for row in range(sz.extent):
            lo = t * sz.rows + row * sz.pitch
            cut = slice(row * sz.extent, (row + 1) * sz.extent)
            reduce_grad[t, cut, :] = total[lo : lo + sz.extent] * slope_one[t, cut, :]
    ahead[0] = product(split(reduce_grad[n - 1]), split(w1[:f, :]), NT)
    behind[0] = product(split(reduce_grad[0]), split(w1[f : 2 * f, :]), NT)
    pairs = [split(reduce_grad[t]) for t in range(n)]
    for lo in range(0, sz.channels, f):
        total = jnp.zeros((f, sz.middle), F32)
        for t in range(n):
            if lo == 0:
                block = take(sz, frames, t + 1, 0, f) if t + 1 < n else from_next[0]
            elif lo == f:
                block = take(sz, frames, t - 1, f, 2 * f) if t > 0 else from_prev[0]
            else:
                block = take(sz, frames, t, lo, lo + f)
            total += product(split(block.T), pairs[t])
        whole[lo : lo + f, :] = total
    if order is None:
        outs[0][...] = whole[...]
    else:
        write_slots(sz, me_ref[0], whole, outs, order)


def end_kernel(sz, reduce_grad, w1, residual, before, after, grad_frames):
    n, f = sz.nframes, sz.folded
    w = split(w1[...])
    for t in range(n):
        back = product(split(reduce_grad[t]), w, NT)
        put(sz, grad_frames, t, residual[t, :, 2 * f :] + back[:, 2 * f :], 2 * f)
        if t + 1 < n:
            put(sz, grad_frames, t + 1, residual[t + 1, :, :f] + back[:, :f])
        if t > 0:
            put(
                sz, grad_frames, t - 1,
                residual[t - 1, :, f : 2 * f] + back[:, f : 2 * f], f,
            )
    put(sz, grad_frames, 0, residual[0, :, :f] + before[0])
    put(sz, grad_frames, n - 1, residual[n - 1, :, f : 2 * f] + after[0], f)


VM = pl.BlockSpec(memory_space=pltpu.VMEM)
SM = pl.BlockSpec(memory_space=pltpu.SMEM)


def call(kernel, outs, ins, scratch=(), scalar=False, flops=0):
    specs = [VM] * len(ins)
    if scalar:
        specs[0] = SM
    moved = sum(4 * math.prod(x.shape) for x in list(ins) + list(outs))
    return pl.pallas_call(
        kernel,
        out_shape=list(outs),
        in_specs=specs,
        out_specs=[VM] * len(outs),
        scratch_shapes=list(scratch),
        compiler_params=pltpu.CompilerParams(vmem_limit_bytes=58 * 1024 * 1024),
        cost_estimate=pl.CostEstimate(flops=flops, bytes_accessed=moved, transcendentals=0),
    )(*ins)


def scatter_sum(sz, pieces, order):
    shards = sz.shards
    if order is None:
        return lax.psum_scatter(pieces[0], "tm", scatter_dimension=0, tiled=True)
    arrived = []
    for stage, piece in enumerate(pieces[:-1]):
        rows = piece.shape[0]
        for block in arrived:
            piece = piece + block[rows : 2 * rows]
        route = [(i, i ^ order[stage]) for i in range(shards)]
        arrived.append(lax.ppermute(piece, "tm", route))
    total = pieces[-1]
    for block in arrived:
        total = total + block[: total.shape[0]]
    return total


def local(
    frames,
    cotangent,
    reduce_weight,
    spatial_weight,
    expand_weight,
    reduce_scale,
    reduce_bias,
    spatial_scale,
    spatial_bias,
    expand_scale,
    expand_bias,
):
    nframes, ncells, channels = frames.shape
    middle = reduce_weight.shape[1]
    shards = lax.axis_size("tm")
    sz = Sizes(nframes, ncells, channels, middle, shards)
    f = sz.folded

    def order_of(total):
        if shards & (shards - 1) or shards == 1 or total % (8 * shards):
            return None
        return [1 << b for b in range(shards.bit_length() - 1)]

    def late_second(order):
        return order if order is None else order[:1] + order[2:] + order[1:2]

    def grads(total):
        if order_of(total) is None:
            return [jax.ShapeDtypeStruct((total, middle), F32)]
        return slot_shapes(sz, total, middle)

    def full(*shape):
        return jax.ShapeDtypeStruct(shape, F32)

    me = lax.axis_index("tm").astype(jnp.int32).reshape(1)
    work = 6 * nframes * ncells * middle
    from_next = passed_along(frames[:1, :, :f], "tm", -1)
    from_prev = passed_along(frames[-1:, :, f : 2 * f], "tm", 1)
    rs, rb, ss, sb, es, eb = [
        x.reshape(1, -1)
        for x in (reduce_scale, reduce_bias, spatial_scale, spatial_bias, expand_scale, expand_bias)
    ]
    frame_rows = view(frames)
    lines = full(*frame_rows.shape)
    (part,) = call(
        functools.partial(begin_kernel, sz),
        [full(nframes, ncells, middle)],
        [frame_rows, reduce_weight],
        flops=work * channels,
    )
    block_out, residual, padded_one, padded_grad, slope_one, flat = call(
        functools.partial(middle_kernel, sz),
        [
            lines,
            full(nframes, ncells, channels),
            full(nframes, sz.tall + 16, middle),
            full(nframes, sz.tall + 16, middle),
            full(nframes, ncells, middle),
            full(nframes, ncells, middle),
        ],
        [part, from_next, from_prev, frame_rows, view(cotangent), reduce_weight, spatial_weight,
         expand_weight, rs, rb, ss, sb, es, eb],
        [
            pltpu.VMEM((3, nframes, sz.tall, middle), BF16),
            pltpu.VMEM((3, nframes, sz.tall, middle), BF16),
        ],
        flops=work * (9 * middle + 2 * channels),
    )
    spatial_order, channel_order = order_of(9 * middle), order_of(channels)
    expand_order = late_second(channel_order)
    spatial_pieces = call(
        functools.partial(spatial_kernel, sz, spatial_order),
        grads(9 * middle),
        [me, padded_one, padded_grad],
        [pltpu.VMEM((9 * middle, middle), F32)],
        scalar=True,
        flops=work * 9 * middle,
    )
    grad_spatial = scatter_sum(sz, spatial_pieces, spatial_order)
    expand_pieces = call(
        functools.partial(expand_kernel, sz, expand_order),
        grads(channels),
        [me, residual, flat, es],
        [pltpu.VMEM((channels, middle), F32)],
        scalar=True,
        flops=work * channels,
    )
    grad_expand = scatter_sum(sz, expand_pieces, expand_order)
    reduce_grad, ahead, behind, *reduce_pieces = call(
        functools.partial(reduce_kernel, sz, channel_order),
        [full(nframes, ncells, middle), full(1, ncells, f), full(1, ncells, f)] + grads(channels),
        [me, padded_grad, slope_one, spatial_weight, reduce_weight, frame_rows, from_next, from_prev],
        [pltpu.VMEM((channels, middle), F32)],
        scalar=True,
        flops=work * (9 * middle + channels),
    )
    before = passed_along(ahead, "tm", 1)
    after = passed_along(behind, "tm", -1)
    grad_reduce = scatter_sum(sz, reduce_pieces, channel_order)
    (grad_frames,) = call(
        functools.partial(end_kernel, sz),
        [lines],
        [reduce_grad, reduce_weight, residual, before, after],
        flops=work * channels,
    )
    return (
        unview(block_out, frames.shape),
        unview(grad_frames, frames.shape),
        grad_reduce,
        grad_spatial,
        grad_expand,
    )


def solution(mesh):
    return jax.shard_map(
        local,
        mesh=mesh,
        in_specs=(
            P(("groups", "tm"), None, None),
            P(("groups", "tm"), None, None),
            P(),
            P(),
            P(),
            P(),
            P(),
            P(),
            P(),
            P(),
            P(),
        ),
        out_specs=(
            P(("groups", "tm"), None, None),
            P(("groups", "tm"), None, None),
            P(("groups", "tm"), None),
            P(("groups", "tm"), None),
            P(("groups", "tm"), None),
        ),
        check_vma=False,
    )
```

```python
import functools
import math

import jax
import jax.numpy as jnp
from jax import lax
from jax.experimental import pallas as pl
from jax.experimental.pallas import tpu as pltpu
from jax.sharding import PartitionSpec as P


F32 = jnp.float32
BF16 = jnp.bfloat16
ROOT = math.sqrt(2.0 / math.pi)
CUBE = 0.044715
NN = (((1,), (0,)), ((), ()))
NT = (((1,), (1,)), ((), ()))


def passed_along(block, axis, distance):
    devices = range(lax.axis_size(axis))
    route = [(i - distance, i) for i in devices if i - distance in devices]
    return lax.ppermute(block, axis, route)


def split(values):
    high = values.astype(BF16)
    low = (values - high.astype(F32)).astype(BF16)
    return high, low


def product(left, right, dims=NN):
    def one(a, b):
        return lax.dot_general(a, b, dims, preferred_element_type=F32)

    return one(left[0], right[0]) + (one(left[0], right[1]) + one(left[1], right[0]))


def gelu_pair(values):
    square = values * values
    half = 0.5 * jnp.tanh(values * ((ROOT * CUBE) * square + ROOT)) + 0.5
    inner = values * ((6.0 * ROOT * CUBE) * square + 2.0 * ROOT)
    return values * half, half * (1.0 + (1.0 - half) * inner)


def pick(pair, index):
    return pair[0][index], pair[1][index]


class Sizes:
    def __init__(self, nframes, ncells, channels, middle, shards):
        self.nframes, self.ncells = nframes, ncells
        self.channels, self.middle, self.shards = channels, middle, shards
        self.extent = math.isqrt(ncells)
        self.pitch = 16
        self.rows = self.extent * self.pitch
        self.tall = (self.extent + 2) * self.pitch
        self.folded = channels // 8


def view(array):
    nframes, ncells, channels = array.shape
    turned = array.transpose(1, 0, 2).reshape(ncells, nframes, channels // 128, 128)
    return turned.transpose(0, 2, 1, 3).reshape(-1, 128)


def unview(rows, shape):
    nframes, ncells, channels = shape
    turned = rows.reshape(ncells, channels // 128, nframes, 128).transpose(0, 2, 1, 3)
    return turned.reshape(ncells, nframes, channels).transpose(1, 0, 2)


def tile_rows(sz, t, tile):
    return pl.ds(sz.nframes * tile + t, sz.ncells, stride=sz.nframes * (sz.channels // 128))


def take(sz, ref, t, lo=0, hi=None):
    hi = sz.channels if hi is None else hi
    tiles = [ref[tile_rows(sz, t, j), :] for j in range(lo // 128, hi // 128)]
    return tiles[0] if len(tiles) == 1 else jnp.concatenate(tiles, axis=1)


def put(sz, ref, t, values, lo=0):
    for j in range(values.shape[1] // 128):
        ref[tile_rows(sz, t, lo // 128 + j), :] = values[:, 128 * j : 128 * (j + 1)]


def to_pitch(sz, target, frame, flat):
    for row in range(sz.extent):
        at = 8 + sz.pitch * (row + 1)
        target[frame, at : at + sz.extent, :] = flat[row * sz.extent : (row + 1) * sz.extent]


def to_flat(sz, target, frame, pitched):
    for row in range(sz.extent):
        target[frame, row * sz.extent : (row + 1) * sz.extent, :] = pitched[
            row * sz.pitch : row * sz.pitch + sz.extent
        ]


def slot_source(slot, order):
    bits = len(order)
    return sum(((slot >> (bits - 1 - b)) & 1) * order[b] for b in range(bits))


def write_slots(sz, me, source, outs, order):
    rows = source.shape[0] // sz.shards
    base = sz.shards
    for out in outs:
        count = out.shape[0] // rows
        base -= count
        for k in range(count):
            chunk = jnp.bitwise_xor(me, slot_source(base + k, order))
            out[k * rows : (k + 1) * rows, :] = source[
                pl.ds(pl.multiple_of(chunk * rows, 8), rows), :
            ]


def slot_shapes(sz, total, width):
    rows = total // sz.shards
    counts, left = [], sz.shards
    while left > 1:
        left //= 2
        counts.append(left)
    counts.append(1)
    return [jax.ShapeDtypeStruct((c * rows, width), F32) for c in counts]


def begin_kernel(sz, frames, weight, part):
    f = sz.folded
    w = split(weight[...])
    for t in range(sz.nframes):
        total = product(split(take(sz, frames, t, 2 * f)), pick(w, slice(2 * f, None)))
        if t + 1 < sz.nframes:
            total += product(split(take(sz, frames, t + 1, 0, f)), pick(w, slice(0, f)))
        if t > 0:
            total += product(split(take(sz, frames, t - 1, f, 2 * f)), pick(w, slice(f, 2 * f)))
        part[t] = total


def middle_kernel(
    sz, part, from_next, from_prev, frames, cotangent, w1, w2, w3,
    rs, rb, ss, sb, es, eb, *refs
):
    block_out, residual, padded_one, padded_grad, slope_one, flat, high, low = refs
    f, n = sz.folded, sz.nframes
    padded_one[...] = jnp.zeros_like(padded_one)
    padded_grad[...] = jnp.zeros_like(padded_grad)
    for t in range(n):
        pre = part[t]
        if t + 1 == n:
            pre += product(split(from_next[0]), split(w1[:f, :]))
        if t == 0:
            pre += product(split(from_prev[0]), split(w1[f : 2 * f, :]))
        hidden, slope = gelu_pair(rs[...] * pre + rb[...])
        slope_one[t] = slope * rs[...]
        to_pitch(sz, padded_one, t, hidden)
    for c in range(3):
        h, l = split(padded_one[:, 7 + c : 7 + c + sz.tall, :])
        high[c], low[c] = h, l
    total = jnp.zeros((n * sz.rows, sz.middle), F32)
    for r in range(3):
        for c in range(3):
            tap = 3 * r + c
            cut = slice(sz.pitch * r, sz.pitch * r + sz.rows)
            left = (
                high[c, :, cut, :].reshape(n * sz.rows, sz.middle),
                low[c, :, cut, :].reshape(n * sz.rows, sz.middle),
            )
            total += product(left, split(w2[tap * sz.middle : (tap + 1) * sz.middle, :]))
    hidden_two, slope_two = gelu_pair(ss[...] * total + sb[...])
    slope_two = slope_two * ss[...]
    w = split(w3[...])
    for t in range(n):
        to_flat(sz, flat, t, hidden_two[t * sz.rows : (t + 1) * sz.rows])
    for t in range(n):
        pre = es[...] * product(split(flat[t]), w, NT) + eb[...] + take(sz, frames, t)
        block, slope = gelu_pair(pre)
        put(sz, block_out, t, block)
        residual[t] = take(sz, cotangent, t) * slope
    for t in range(n):
        grad = residual[t] * es[...]
        back = product(split(grad), w)
        for row in range(sz.extent):
            at = 8 + sz.pitch * (row + 1)
            lo = t * sz.rows + row * sz.pitch
            padded_grad[t, at : at + sz.extent, :] = (
                back[row * sz.extent : (row + 1) * sz.extent]
                * slope_two[lo : lo + sz.extent]
            )


def expand_kernel(sz, order, me_ref, residual, flat, es, *refs):
    outs, (whole,) = refs[:-1], refs[-1:]
    pairs = [split(flat[t]) for t in range(sz.nframes)]
    step = 256
    for lo in range(0, sz.channels, step):
        total = jnp.zeros((step, sz.middle), F32)
        for t in range(sz.nframes):
            grad = residual[t, :, lo : lo + step] * es[:, lo : lo + step]
            total += product(split(grad.T), pairs[t])
        whole[lo : lo + step, :] = total
    if order is None:
        outs[0][...] = whole[...]
    else:
        write_slots(sz, me_ref[0], whole, outs, order)


def shifted_grads(sz, padded_grad, c):
    return split(padded_grad[:, 9 - c : 9 - c + sz.tall, :])


def spatial_kernel(sz, order, me_ref, padded_one, padded_grad, *refs):
    outs, (whole,) = refs[:-1], refs[-1:]
    n = sz.nframes
    at = 8 + sz.pitch
    turned = split(
        padded_one[:, at : at + sz.rows, :].reshape(n * sz.rows, sz.middle).T
    )
    for c in range(3):
        pair = shifted_grads(sz, padded_grad, c)
        for r in range(3):
            tap = 3 * r + c
            cut = slice(sz.pitch * (2 - r), sz.pitch * (2 - r) + sz.rows)
            right = tuple(x[:, cut, :].reshape(n * sz.rows, sz.middle) for x in pair)
            whole[tap * sz.middle : (tap + 1) * sz.middle, :] = product(turned, right)
    if order is None:
        outs[0][...] = whole[...]
    else:
        write_slots(sz, me_ref[0], whole, outs, order)


def reduce_kernel(
    sz, order, me_ref, padded_grad, slope_one, w2, w1, frames, from_next, from_prev, *refs
):
    reduce_grad, ahead, behind = refs[:3]
    outs, (whole,) = refs[3:-1], refs[-1:]
    n, f = sz.nframes, sz.folded
    total = jnp.zeros((n * sz.rows, sz.middle), F32)
    for c in range(3):
        pair = shifted_grads(sz, padded_grad, c)
        for r in range(3):
            tap = 3 * r + c
            cut = slice(sz.pitch * (2 - r), sz.pitch * (2 - r) + sz.rows)
            left = tuple(x[:, cut, :].reshape(n * sz.rows, sz.middle) for x in pair)
            total += product(left, split(w2[tap * sz.middle : (tap + 1) * sz.middle, :]), NT)
    for t in range(n):
        for row in range(sz.extent):
            lo = t * sz.rows + row * sz.pitch
            cut = slice(row * sz.extent, (row + 1) * sz.extent)
            reduce_grad[t, cut, :] = total[lo : lo + sz.extent] * slope_one[t, cut, :]
    ahead[0] = product(split(reduce_grad[n - 1]), split(w1[:f, :]), NT)
    behind[0] = product(split(reduce_grad[0]), split(w1[f : 2 * f, :]), NT)
    pairs = [split(reduce_grad[t]) for t in range(n)]
    for lo in range(0, sz.channels, f):
        total = jnp.zeros((f, sz.middle), F32)
        for t in range(n):
            if lo == 0:
                block = take(sz, frames, t + 1, 0, f) if t + 1 < n else from_next[0]
            elif lo == f:
                block = take(sz, frames, t - 1, f, 2 * f) if t > 0 else from_prev[0]
            else:
                block = take(sz, frames, t, lo, lo + f)
            total += product(split(block.T), pairs[t])
        whole[lo : lo + f, :] = total
    if order is None:
        outs[0][...] = whole[...]
    else:
        write_slots(sz, me_ref[0], whole, outs, order)


def end_kernel(sz, reduce_grad, w1, residual, before, after, grad_frames):
    n, f = sz.nframes, sz.folded
    w = split(w1[...])
    for t in range(n):
        back = product(split(reduce_grad[t]), w, NT)
        put(sz, grad_frames, t, residual[t, :, 2 * f :] + back[:, 2 * f :], 2 * f)
        if t + 1 < n:
            put(sz, grad_frames, t + 1, residual[t + 1, :, :f] + back[:, :f])
        if t > 0:
            put(
                sz, grad_frames, t - 1,
                residual[t - 1, :, f : 2 * f] + back[:, f : 2 * f], f,
            )
    put(sz, grad_frames, 0, residual[0, :, :f] + before[0])
    put(sz, grad_frames, n - 1, residual[n - 1, :, f : 2 * f] + after[0], f)


VM = pl.BlockSpec(memory_space=pltpu.VMEM)
SM = pl.BlockSpec(memory_space=pltpu.SMEM)


def call(kernel, outs, ins, scratch=(), scalar=False, flops=0):
    specs = [VM] * len(ins)
    if scalar:
        specs[0] = SM
    moved = sum(4 * math.prod(x.shape) for x in list(ins) + list(outs))
    return pl.pallas_call(
        kernel,
        out_shape=list(outs),
        in_specs=specs,
        out_specs=[VM] * len(outs),
        scratch_shapes=list(scratch),
        compiler_params=pltpu.CompilerParams(vmem_limit_bytes=58 * 1024 * 1024),
        cost_estimate=pl.CostEstimate(flops=flops, bytes_accessed=moved, transcendentals=0),
    )(*ins)


def scatter_sum(sz, pieces, order):
    shards = sz.shards
    if order is None:
        return lax.psum_scatter(pieces[0], "tm", scatter_dimension=0, tiled=True)
    arrived = []
    for stage, piece in enumerate(pieces[:-1]):
        rows = piece.shape[0]
        for block in arrived:
            piece = piece + block[rows : 2 * rows]
        route = [(i, i ^ order[stage]) for i in range(shards)]
        arrived.append(lax.ppermute(piece, "tm", route))
    total = pieces[-1]
    for block in arrived:
        total = total + block[: total.shape[0]]
    return total


def local(
    frames,
    cotangent,
    reduce_weight,
    spatial_weight,
    expand_weight,
    reduce_scale,
    reduce_bias,
    spatial_scale,
    spatial_bias,
    expand_scale,
    expand_bias,
):
    nframes, ncells, channels = frames.shape
    middle = reduce_weight.shape[1]
    shards = lax.axis_size("tm")
    sz = Sizes(nframes, ncells, channels, middle, shards)
    f = sz.folded

    def order_of(total):
        if shards & (shards - 1) or shards == 1 or total % (8 * shards):
            return None
        return [1 << b for b in range(shards.bit_length() - 1)]

    def late_second(order):
        return order if order is None else order[:1] + order[2:3] + order[1:2] + order[3:]

    def grads(total):
        if order_of(total) is None:
            return [jax.ShapeDtypeStruct((total, middle), F32)]
        return slot_shapes(sz, total, middle)

    def full(*shape):
        return jax.ShapeDtypeStruct(shape, F32)

    me = lax.axis_index("tm").astype(jnp.int32).reshape(1)
    work = 6 * nframes * ncells * middle
    from_next = passed_along(frames[:1, :, :f], "tm", -1)
    from_prev = passed_along(frames[-1:, :, f : 2 * f], "tm", 1)
    rs, rb, ss, sb, es, eb = [
        x.reshape(1, -1)
        for x in (reduce_scale, reduce_bias, spatial_scale, spatial_bias, expand_scale, expand_bias)
    ]
    frame_rows = view(frames)
    lines = full(*frame_rows.shape)
    (part,) = call(
        functools.partial(begin_kernel, sz),
        [full(nframes, ncells, middle)],
        [frame_rows, reduce_weight],
        flops=work * channels,
    )
    block_out, residual, padded_one, padded_grad, slope_one, flat = call(
        functools.partial(middle_kernel, sz),
        [
            lines,
            full(nframes, ncells, channels),
            full(nframes, sz.tall + 16, middle),
            full(nframes, sz.tall + 16, middle),
            full(nframes, ncells, middle),
            full(nframes, ncells, middle),
        ],
        [part, from_next, from_prev, frame_rows, view(cotangent), reduce_weight, spatial_weight,
         expand_weight, rs, rb, ss, sb, es, eb],
        [
            pltpu.VMEM((3, nframes, sz.tall, middle), BF16),
            pltpu.VMEM((3, nframes, sz.tall, middle), BF16),
        ],
        flops=work * (9 * middle + 2 * channels),
    )
    spatial_order, channel_order = order_of(9 * middle), order_of(channels)
    expand_order = late_second(channel_order)
    spatial_pieces = call(
        functools.partial(spatial_kernel, sz, spatial_order),
        grads(9 * middle),
        [me, padded_one, padded_grad],
        [pltpu.VMEM((9 * middle, middle), F32)],
        scalar=True,
        flops=work * 9 * middle,
    )
    grad_spatial = scatter_sum(sz, spatial_pieces, spatial_order)
    expand_pieces = call(
        functools.partial(expand_kernel, sz, expand_order),
        grads(channels),
        [me, residual, flat, es],
        [pltpu.VMEM((channels, middle), F32)],
        scalar=True,
        flops=work * channels,
    )
    grad_expand = scatter_sum(sz, expand_pieces, expand_order)
    reduce_grad, ahead, behind, *reduce_pieces = call(
        functools.partial(reduce_kernel, sz, channel_order),
        [full(nframes, ncells, middle), full(1, ncells, f), full(1, ncells, f)] + grads(channels),
        [me, padded_grad, slope_one, spatial_weight, reduce_weight, frame_rows, from_next, from_prev],
        [pltpu.VMEM((channels, middle), F32)],
        scalar=True,
        flops=work * (9 * middle + channels),
    )
    before = passed_along(ahead, "tm", 1)
    after = passed_along(behind, "tm", -1)
    grad_reduce = scatter_sum(sz, reduce_pieces, channel_order)
    (grad_frames,) = call(
        functools.partial(end_kernel, sz),
        [lines],
        [reduce_grad, reduce_weight, residual, before, after],
        flops=work * channels,
    )
    return (
        unview(block_out, frames.shape),
        unview(grad_frames, frames.shape),
        grad_reduce,
        grad_spatial,
        grad_expand,
    )


def solution(mesh):
    return jax.shard_map(
        local,
        mesh=mesh,
        in_specs=(
            P(("groups", "tm"), None, None),
            P(("groups", "tm"), None, None),
            P(),
            P(),
            P(),
            P(),
            P(),
            P(),
            P(),
            P(),
            P(),
        ),
        out_specs=(
            P(("groups", "tm"), None, None),
            P(("groups", "tm"), None, None),
            P(("groups", "tm"), None),
            P(("groups", "tm"), None),
            P(("groups", "tm"), None),
        ),
        check_vma=False,
    )
```
